32 devices in a mesh: replica: 4 (over y, core), dp: 8 (over z, x).
Axes of the slice: x: 2, y: 2, z: 4, core: 2. Of those that a mesh axis runs over, the one named last changes fastest.
Arguments:
- features: bfloat16 [3072, 256], P('dp'), may hold values from -160 to 160
- prototypes: bfloat16 [256, 131072], P(None, ('replica', 'dp')), may hold values from -120 to 120
Outputs:
- codes: bfloat16 [3072, 131072], P('dp', 'replica')
The draws below stay inside these ranges and needn't reach their ends.
All inputs are finite; a program needn't handle non-finite values.
Results may differ from the reference program's by a relative error of at most 0.0058.
Values may be sent and summed in bfloat16 or wider, within the bound.
No kernel may reach another device: no remote copies, remote signals or barrier semaphores. Data moves between devices by JAX's collectives and lax.ppermute only.
A program may use at most 192 MiB of HBM per device.

```python
import math
import jax
import jax.numpy as jnp
from jax import lax

D = 256
PROTOS = 131072
ITERS = 3
BATCH = 3072


cluster_count = 16


def cluster_directions(key):
    return jnp.clip(jax.random.normal(jax.random.fold_in(key, 7), (cluster_count, D), jnp.float32), -4.0, 4.0)


def draw_features(key, part):
    directions = cluster_directions(key)
    first_pick = jax.random.randint(jax.random.fold_in(key, 14), (BATCH,), 0, cluster_count)
    second_pick = jax.random.randint(jax.random.fold_in(key, 15), (BATCH,), 0, cluster_count)
    membership = jnp.minimum(first_pick, second_pick)
    own_direction = directions[membership]
    jitter = jnp.clip(jax.random.normal(jax.random.fold_in(key, 11), (BATCH, D), jnp.float32), -4.0, 4.0)
    loading = jax.random.uniform(jax.random.fold_in(key, 12), (BATCH, 1), jnp.float32, 0.0, 2.0)
    scales = jnp.exp(jax.random.uniform(jax.random.fold_in(key, 13), (BATCH, 1), jnp.float32, 0.0, math.log(10.0)))
    return (scales * (jitter + loading * own_direction)).astype(jnp.bfloat16)


def draw_prototypes(key, part):
    directions = cluster_directions(key)
    membership = jax.random.randint(jax.random.fold_in(key, 24), (PROTOS,), 0, cluster_count)
    own_direction = directions[membership].T
    jitter = jnp.clip(jax.random.normal(jax.random.fold_in(key, 21), (D, PROTOS), jnp.float32), -4.0, 4.0)
    column_tilt = jax.random.uniform(jax.random.fold_in(key, 22), (1, PROTOS), jnp.float32, -1.5, 1.5)
    scales = jnp.exp(jax.random.uniform(jax.random.fold_in(key, 23), (1, PROTOS), jnp.float32, 0.0, math.log(10.0)))
    return (scales * (jitter + column_tilt * own_direction)).astype(jnp.bfloat16)


def setup_inputs(seed: int = 0) -> dict:
    key_of = jax.random.split(jax.random.key(seed), 3)
    features = draw_features(jax.random.fold_in(key_of[2], 71), 0)
    prototypes = draw_prototypes(jax.random.fold_in(key_of[2], 71), 0)
    return {"features": features, "prototypes": prototypes}


epsilon = 1e-06
sharpness_divisor = 0.07

def unit_rows(values):
    return values * lax.rsqrt(lax.optimization_barrier(jnp.sum(values * values, axis=1, keepdims=True)) + epsilon)

def unit_columns(values):
    return values * lax.rsqrt(lax.optimization_barrier(jnp.sum(values * values, axis=0, keepdims=True)) + epsilon)

def exponentials(normalised_embeddings, column_block):
    tempered_scores = unit_columns(column_block.astype(jnp.float32)).astype(jnp.bfloat16)
    scores = jnp.dot(normalised_embeddings, tempered_scores, preferred_element_type=jnp.float32)
    return jnp.exp(scores / sharpness_divisor).astype(jnp.bfloat16)

def reference(features, prototypes):
    normalised_embeddings = unit_rows(features.astype(jnp.float32)).astype(jnp.bfloat16)
    block_width = min(PROTOS, 4096)
    block_count = PROTOS // block_width
    stacked = prototypes.reshape(D, block_count, block_width).transpose(1, 0, 2)

    def make_block(column_block):
        return exponentials(normalised_embeddings, column_block)
    kernel_blocks = lax.map(make_block, stacked)
    row_scale_factors = jnp.ones((BATCH,), jnp.float32)
    cols_scale = jnp.ones((block_count, block_width), jnp.float32)
    for iteration in range(ITERS):
        rounded_rows = row_scale_factors.astype(jnp.bfloat16)

        def column_totals(block):
            return jnp.dot(rounded_rows, block, preferred_element_type=jnp.float32)
        cols_scale = 1.0 / lax.map(column_totals, kernel_blocks)
        rounded_cols = cols_scale.astype(jnp.bfloat16)

        def row_terms(pair):
            return jnp.dot(pair[0], pair[1], preferred_element_type=jnp.float32)
        row_scale_factors = 1.0 / lax.optimization_barrier(jnp.sum(lax.map(row_terms, (kernel_blocks, rounded_cols)), axis=0))
    codes = (PROTOS * kernel_blocks.astype(jnp.float32) * row_scale_factors[None, :, None] * cols_scale[:, None, :]).astype(jnp.bfloat16)
    return codes.transpose(1, 0, 2).reshape(BATCH, PROTOS)
```

```python
import jax
import jax.numpy as jnp
from jax import lax
from jax.sharding import PartitionSpec as P

PROTOS = 131072
ITERS = 3


epsilon = 1e-06
sharpness_divisor = 0.07


def unit_rows(values):
    return values * lax.rsqrt(jnp.sum(values * values, axis=1, keepdims=True) + epsilon)


def unit_columns(values):
    return values * lax.rsqrt(jnp.sum(values * values, axis=0, keepdims=True) + epsilon)


def kernel_of(features, prototypes):
    normed = unit_rows(features.astype(jnp.float32)).astype(jnp.bfloat16)
    unit = unit_columns(prototypes.astype(jnp.float32)).astype(jnp.bfloat16)
    scores = jnp.dot(normed, unit, preferred_element_type=jnp.float32)
    return jnp.exp(scores / sharpness_divisor).astype(jnp.bfloat16)


def local(features, prototypes):
    rows = features.shape[0]
    mine = kernel_of(lax.all_gather(features, "dp", axis=0, tiled=True), prototypes)
    row_scale = jnp.ones((mine.shape[0],), jnp.float32)
    for _ in range(ITERS):
        col_scale = 1.0 / jnp.dot(row_scale.astype(jnp.bfloat16), mine, preferred_element_type=jnp.float32)
        partial = jnp.dot(mine, col_scale.astype(jnp.bfloat16), preferred_element_type=jnp.float32)
        row_scale = 1.0 / lax.psum(partial, ("dp", "replica"))
    col_scale = lax.all_gather(col_scale, "dp", axis=0, tiled=True)
    row_scale = lax.dynamic_slice_in_dim(row_scale, lax.axis_index("dp") * rows, rows)
    entries = kernel_of(features, lax.all_gather(prototypes, "dp", axis=1, tiled=True))
    return (
        PROTOS * entries.astype(jnp.float32) * row_scale[:, None] * col_scale[None, :]
    ).astype(jnp.bfloat16)


def solution(mesh):
    placed = (P("dp", None), P(None, ("replica", "dp")))
    return jax.shard_map(
        local, mesh=mesh, in_specs=placed, out_specs=P("dp", "replica"), check_vma=False
    )
```
